32 devices in a mesh: dp: 8 (over z, y), sub: 4 (over x, core).
Axes of the slice: x: 2, y: 2, z: 4, core: 2. Of those that a mesh axis runs over, the one named last changes fastest.
Arguments:
- tokens: bfloat16 [32768, 768], P(('dp', 'sub')), may hold values from -6 to 6
- segment_ids: int32 [32768], P(('dp', 'sub')), may hold values from 0 to 511, as said below
- positions: int32 [32768], P(('dp', 'sub')), may hold values from 0 to 511, as said below
- out_grad: bfloat16 [32768, 768], P(('dp', 'sub')), may hold values from -6 to 6
- w_query: bfloat16 [768, 768], replicated, may hold values from -0.21875 to 0.21875
- w_key: bfloat16 [768, 768], replicated, may hold values from -0.21875 to 0.21875
- w_value: bfloat16 [768, 768], replicated, may hold values from -0.21875 to 0.21875
- w_out: bfloat16 [768, 768], replicated, may hold values from -0.3125 to 0.3125
- w_up: bfloat16 [768, 3072], replicated, may hold values from -0.21875 to 0.21875
- b_up: float32 [3072], replicated, may hold values from -3 to 3
- w_down: bfloat16 [3072, 768], replicated, may hold values from -0.15625 to 0.15625
- b_down: float32 [768], replicated, may hold values from -3 to 3
- gain_attn: float32 [768], replicated, may hold values from 0.1 to 1.9
- gain_mlp: float32 [768], replicated, may hold values from 0.1 to 1.9
Outputs:
- layer_out: bfloat16 [32768, 768], P(('dp', 'sub'))
- grad_tokens: bfloat16 [32768, 768], P(('dp', 'sub'))
- grad_query: float32 [768, 768], replicated
- grad_key: float32 [768, 768], replicated
- grad_value: float32 [768, 768], replicated
- grad_outproj: float32 [768, 768], replicated
- grad_up: float32 [768, 3072], replicated
- grad_upbias: float32 [3072], replicated
- grad_down: float32 [3072, 768], replicated
- grad_downbias: float32 [768], replicated
- grad_gainattn: float32 [768], replicated
- grad_gainmlp: float32 [768], replicated
The draws below stay inside these ranges and needn't reach their ends.
Inputs may be any that keep to these rules, and one draw needn't show every extreme that they name: `segment_ids`: tokens come in aligned blocks of 512; a token's id is the block-local index of the first token of its series, so ids repeat from block to block and no series crosses a block's edge. A series has 1 to 64 tokens; every block holds one series of exactly 64 tokens, and its last token is a series of one. Within a series positions rise by one from token to token, beginning anywhere from 0 to 448; each block's series of 64 tokens ends at position 511.
All inputs are finite; a program needn't handle non-finite values.
Results may differ from the reference program's by a relative error of at most 0.011.
Values sent between devices are 32-bit elements; how exact they have to be, the bound alone decides.
No kernel may reach another device: no remote copies, remote signals or barrier semaphores. Data moves between devices by JAX's collectives and lax.ppermute only.
A program may use at most 192 MiB of HBM per device.

```python
import math
import jax
import jax.numpy as jnp
from jax import lax

D = 768
HEADS = 12
HEAD = 64
A = 768
FF = 3072
BLK = 512
SERIES_MOST = 64
TOKENS = 32768


def packing(key):
    base = jax.random.fold_in(key, 31)
    key_coin, key_start, key_length, key_long, key_offset = jax.random.split(base, 5)
    block_count = TOKENS // BLK
    places = jnp.arange(BLK, dtype=jnp.int32)[None, :]
    coin = jax.random.randint(key_coin, (block_count, BLK), 0, 2) == 1
    forced = places % (SERIES_MOST // 2) == 0
    clear_start = jax.random.randint(key_start, (block_count, 4, 1), 0, BLK)
    clear_length = jax.random.randint(key_length, (block_count, 4, 1), SERIES_MOST // 8, SERIES_MOST // 2)
    cleared = jnp.any((places[:, None, :] >= clear_start) & (places[:, None, :] < clear_start + clear_length), axis=1)
    flags = coin & jnp.logical_not(cleared) | forced
    long_start = jax.random.randint(key_long, (block_count, 1), 0, BLK - SERIES_MOST)
    inside = (places > long_start) & (places < long_start + SERIES_MOST)
    flags = jnp.where(inside, False, flags)
    flags = flags | (places == long_start) | (places == long_start + SERIES_MOST) | (places == 0) | (places == BLK - 1)
    starts = lax.cummax(jnp.where(flags, places, 0), axis=1).astype(jnp.int32)
    offsets = jax.random.randint(key_offset, (block_count, BLK), 0, BLK - SERIES_MOST + 1)
    offsets = jnp.where(places == 0, 0, offsets)
    offsets = jnp.where(places == long_start, BLK - SERIES_MOST, offsets)
    first_place = jnp.take_along_axis(offsets, starts, axis=1)
    positions = (places - starts + first_place).astype(jnp.int32)
    return (starts.reshape(-1), positions.reshape(-1))


def draw_segment_ids(key, part):
    return packing(key)[0]


def draw_positions(key, part):
    return packing(key)[1]


def block_levels(own_key, extent, shards, least, largest):
    factor_of, own = 1.0, jax.random.fold_in(own_key, 6)
    for position, shards_of in shards:
        steps = jnp.exp(jax.random.uniform(jax.random.fold_in(own, position), (shards_of,), jnp.float32, least / len(shards), largest / len(shards)))
        factor_of = factor_of * jnp.repeat(steps, extent[position] // shards_of).reshape([-1 if axis == position else 1 for axis in range(len(extent))])
    return factor_of


def bell_draw(stream_key, extent, width, limit, cuts=(), held_as=jnp.bfloat16):
    values = width * jax.random.normal(stream_key, extent, jnp.float32)
    if cuts:
        values = values * block_levels(stream_key, extent, cuts, -0.22, 0.18)
    return jnp.clip(values, -limit, limit).astype(held_as)


def setup_inputs(seed: int = 0) -> dict:
    keys = jax.random.split(jax.random.key(seed), 15)
    return {
        "tokens": bell_draw(keys[0], (TOKENS, D), 1.0, 6.0, ((0, 32),)),
        "segment_ids": draw_segment_ids(jax.random.fold_in(keys[14], 71), 0),
        "positions": draw_positions(jax.random.fold_in(keys[14], 71), 0),
        "out_grad": bell_draw(keys[3], (TOKENS, D), 1.0, 6.0, ((0, 32),)),
        "w_query": bell_draw(keys[4], (D, A), D ** -0.5, 0.21875),
        "w_key": bell_draw(keys[5], (D, A), D ** -0.5, 0.21875),
        "w_value": bell_draw(keys[6], (D, A), D ** -0.5, 0.21875),
        "w_out": bell_draw(keys[7], (A, D), (A // 2) ** -0.5, 0.3125),
        "w_up": bell_draw(keys[8], (D, FF), D ** -0.5, 0.21875),
        "b_up": bell_draw(keys[9], (FF,), 0.5, 3.0, (), jnp.float32),
        "w_down": bell_draw(keys[10], (FF, D), (FF // 2) ** -0.5, 0.15625),
        "b_down": bell_draw(keys[11], (D,), 0.5, 3.0, (), jnp.float32),
        "gain_attn": jnp.clip(1.0 + 0.18 * jax.random.normal(keys[12], (D,), jnp.float32), 0.1, 1.9),
        "gain_mlp": jnp.clip(1.0 + 0.18 * jax.random.normal(keys[13], (D,), jnp.float32), 0.1, 1.9),
    }


@jax.custom_vjp
def low(v):
    return lax.optimization_barrier(v.astype(jnp.bfloat16)).astype(jnp.float32)

@jax.custom_vjp
def low_back(v):
    return v

def low_keep(v):
    return (low(v), None)

def low_pass(kept, grad):
    return (grad,)

def back_keep(v):
    return (v, None)

def back_low(kept, grad):
    return (low(grad),)
low.defvjp(low_keep, low_pass)
low_back.defvjp(back_keep, back_low)
EPSILON = 1e-06
HIGHEST = lax.Precision.HIGHEST

def tables(positions, head_dim):
    half_dim = head_dim // 2
    frequency = jnp.exp(jnp.arange(half_dim, dtype=jnp.float32) * (-math.log(10000.0) / half_dim))
    phases = positions.astype(jnp.float32)[:, None] * frequency[None, :]
    return (jnp.cos(phases)[:, None, :], jnp.sin(phases)[:, None, :])

def rotate(vectors, cos_table, sin_table):
    half_dim = vectors.shape[-1] // 2
    leading = vectors[..., :half_dim]
    trailing = vectors[..., half_dim:]
    return jnp.concatenate([leading * cos_table - trailing * sin_table, leading * sin_table + trailing * cos_table], axis=-1)

def allowed_pairs(labels):
    places = jnp.arange(labels.shape[0], dtype=jnp.int32)
    return (labels[:, None] == labels[None, :]) & (places[None, :] <= places[:, None])

def attend(pieces):
    queries, key_rows, values, labels = pieces
    scores = low_back(jnp.einsum('qhe,khe->hqk', queries, key_rows, precision=HIGHEST))
    masked = jnp.where(allowed_pairs(labels)[None], scores, -1e+30)
    highest = lax.optimization_barrier(jnp.max(masked, axis=-1, keepdims=True))
    weights = jnp.exp(masked - highest)
    shares = weights / lax.optimization_barrier(jnp.sum(weights, axis=-1, keepdims=True))
    return jnp.einsum('hqk,khe->qhe', low(shares), values, precision=HIGHEST)

def layer(inputs, params, cos_table, sin_table, labels):
    w_query, w_key, w_value, w_out, w_up, b_up, w_down, b_down, gain_attn, gain_mlp = params
    rows = inputs.shape[0]
    blocks = rows // BLK
    scale_attn = lax.rsqrt(lax.optimization_barrier(jnp.mean(inputs * inputs, axis=-1, keepdims=True)) + EPSILON)
    normed_attn = low(inputs * scale_attn * gain_attn)
    query_raw = low_back(jnp.dot(normed_attn, w_query, precision=HIGHEST)).reshape(rows, HEADS, HEAD)
    key_raw = low_back(jnp.dot(normed_attn, w_key, precision=HIGHEST)).reshape(rows, HEADS, HEAD)
    queries = low(rotate(query_raw, cos_table, sin_table) * (1.0 / math.sqrt(HEAD)))
    key_rows = low(rotate(key_raw, cos_table, sin_table))
    values = low(low_back(jnp.dot(normed_attn, w_value, precision=HIGHEST))).reshape(rows, HEADS, HEAD)
    mixed = lax.map(jax.checkpoint(attend), (queries.reshape(blocks, BLK, HEADS, HEAD), key_rows.reshape(blocks, BLK, HEADS, HEAD), values.reshape(blocks, BLK, HEADS, HEAD), labels.reshape(blocks, BLK)))
    attended = low_back(low(mixed.reshape(rows, HEADS * HEAD)))
    residual = inputs + low_back(jnp.dot(attended, w_out, precision=HIGHEST))
    scale_mlp = lax.rsqrt(lax.optimization_barrier(jnp.mean(residual * residual, axis=-1, keepdims=True)) + EPSILON)
    normed_mlp = low(residual * scale_mlp * gain_mlp)
    hidden = low_back(jnp.dot(normed_mlp, w_up, precision=HIGHEST) + b_up)
    activated = low(jax.nn.gelu(hidden, approximate=True))
    return residual + low_back(jnp.dot(activated, w_down, precision=HIGHEST) + b_down)

def reference(tokens, segment_ids, positions, out_grad, w_query, w_key, w_value, w_out, w_up, b_up, w_down, b_down, gain_attn, gain_mlp):
    inputs = tokens.astype(jnp.float32)
    params = (w_query.astype(jnp.float32), w_key.astype(jnp.float32), w_value.astype(jnp.float32), w_out.astype(jnp.float32), w_up.astype(jnp.float32), b_up.astype(jnp.float32), w_down.astype(jnp.float32), b_down.astype(jnp.float32), gain_attn.astype(jnp.float32), gain_mlp.astype(jnp.float32))
    cos_table, sin_table = tables(positions, HEAD)
    block_count = inputs.shape[0] // BLK
    group_blocks = math.gcd(block_count, 8)
    group_rows = group_blocks * BLK
    group_count = block_count // group_blocks
    half_dim = HEAD // 2

    def whole_layer(layer_in, layer_params):

        def group_step(carried, pieces):
            return (carried, jax.checkpoint(layer)(pieces[0], layer_params, pieces[1], pieces[2], pieces[3]))
        carried, outputs = lax.scan(group_step, jnp.zeros((), jnp.float32), (layer_in.reshape(group_count, group_rows, D), cos_table.reshape(group_count, group_rows, 1, half_dim), sin_table.reshape(group_count, group_rows, 1, half_dim), segment_ids.reshape(group_count, group_rows)))
        return outputs.reshape(layer_in.shape)
    layer_out, pullback = jax.vjp(whole_layer, inputs, params)
    grad_inputs, grads = pullback(out_grad.astype(jnp.float32))
    return (layer_out.astype(jnp.bfloat16), grad_inputs.astype(jnp.bfloat16), grads[0], grads[1], grads[2], grads[3], grads[4], grads[5], grads[6], grads[7], grads[8], grads[9])
```

```python
import math

import jax
import jax.numpy as jnp
from jax import lax
from jax.sharding import PartitionSpec as P

HEAD = 64
BLK = 512


EPSILON = 1e-06


def tables(positions, head_dim):
    half_dim = head_dim // 2
    frequency = jnp.exp(jnp.arange(half_dim, dtype=jnp.float32) * (-math.log(10000.0) / half_dim))
    phases = positions.astype(jnp.float32)[:, None] * frequency[None, :]
    return (jnp.cos(phases)[:, None, :], jnp.sin(phases)[:, None, :])


def rotate(vectors, cos_table, sin_table):
    half_dim = vectors.shape[-1] // 2
    leading = vectors[..., :half_dim]
    trailing = vectors[..., half_dim:]
    return jnp.concatenate(
        [leading * cos_table - trailing * sin_table, leading * sin_table + trailing * cos_table],
        axis=-1,
    )


def rotate_back(vectors, cos_table, sin_table):
    half_dim = vectors.shape[-1] // 2
    leading = vectors[..., :half_dim]
    trailing = vectors[..., half_dim:]
    return jnp.concatenate(
        [leading * cos_table + trailing * sin_table, trailing * cos_table - leading * sin_table],
        axis=-1,
    )


def allowed_pairs(labels):
    places = jnp.arange(labels.shape[0], dtype=jnp.int32)
    return (labels[:, None] == labels[None, :]) & (places[None, :] <= places[:, None])


def tanh_gelu(values):
    return jax.nn.gelu(values, approximate=True)


def attend_block(pieces):
    queries, key_rows, values, labels = pieces
    scores = jnp.einsum("qhe,khe->hqk", queries, key_rows, preferred_element_type=jnp.float32)
    masked = jnp.where(allowed_pairs(labels)[None], scores, -1e30)
    highest = jnp.max(masked, axis=-1, keepdims=True)
    weights = jnp.exp(masked - highest)
    totals = jnp.sum(weights, axis=-1, keepdims=True)
    shares = (weights / totals).astype(jnp.bfloat16)
    mixed = jnp.einsum("hqk,khe->qhe", shares, values, preferred_element_type=jnp.float32)
    return (mixed.astype(jnp.bfloat16), highest + jnp.log(totals))


def attend_back(pieces):
    queries, key_rows, values, labels, grad_mixed, log_totals = pieces
    scores = jnp.einsum("qhe,khe->hqk", queries, key_rows, preferred_element_type=jnp.float32)
    masked = jnp.where(allowed_pairs(labels)[None], scores, -1e30)
    shares = jnp.exp(masked - log_totals)
    grad_shares = jnp.einsum("qhe,khe->hqk", grad_mixed, values, preferred_element_type=jnp.float32)
    grad_values = jnp.einsum(
        "hqk,qhe->khe", shares.astype(jnp.bfloat16), grad_mixed, preferred_element_type=jnp.float32
    )
    row_dots = jnp.sum(grad_shares * shares, axis=-1, keepdims=True)
    grad_scores = (shares * (grad_shares - row_dots)).astype(jnp.bfloat16)
    grad_queries = jnp.einsum(
        "hqk,khe->qhe", grad_scores, key_rows, preferred_element_type=jnp.float32
    )
    grad_keys = jnp.einsum("hqk,qhe->khe", grad_scores, queries, preferred_element_type=jnp.float32)
    return (grad_queries, grad_keys, grad_values)


def norm_back(inputs, scale, gain, grad_normed):
    weighted = grad_normed * gain
    grad_inputs = scale * weighted - inputs * (scale * scale * scale) * jnp.mean(
        weighted * inputs, axis=-1, keepdims=True
    )
    grad_gain = jnp.sum(grad_normed * (inputs * scale), axis=0)
    return (grad_inputs, grad_gain)


def summed(grad_query, grad_key, grad_value, grad_outproj, grad_up, grad_upbias, grad_down):
    everywhere = ("dp", "sub")
    return tuple(
        lax.psum(piece, everywhere)
        for piece in (
            grad_query,
            grad_key,
            grad_value,
            grad_outproj,
            grad_up,
            grad_upbias,
            grad_down,
        )
    )


def body(
    tokens,
    segment_ids,
    positions,
    out_grad,
    w_query,
    w_key,
    w_value,
    w_out,
    w_up,
    b_up,
    w_down,
    b_down,
    gain_attn,
    gain_mlp,
):
    rows = tokens.shape[0]
    width = w_query.shape[1]
    head_dim = HEAD
    heads = width // head_dim
    blocks = rows // BLK
    scaling = 1.0 / math.sqrt(head_dim)

    def by_block(array):
        return array.reshape((blocks, BLK) + array.shape[1:])

    cos_table, sin_table = tables(positions, head_dim)
    labels = segment_ids.reshape(blocks, BLK)
    inputs = tokens.astype(jnp.float32)
    scale_attn = lax.rsqrt(jnp.mean(inputs * inputs, axis=-1, keepdims=True) + EPSILON)
    normed_attn = (inputs * scale_attn * gain_attn).astype(jnp.bfloat16)
    query_raw = jnp.dot(normed_attn, w_query, preferred_element_type=jnp.float32).reshape(
        rows, heads, head_dim
    )
    key_raw = jnp.dot(normed_attn, w_key, preferred_element_type=jnp.float32).reshape(
        rows, heads, head_dim
    )
    queries = (rotate(query_raw, cos_table, sin_table) * scaling).astype(jnp.bfloat16)
    key_rows = rotate(key_raw, cos_table, sin_table).astype(jnp.bfloat16)
    values = (
        jnp.dot(normed_attn, w_value, preferred_element_type=jnp.float32)
        .astype(jnp.bfloat16)
        .reshape(rows, heads, head_dim)
    )
    mixed, log_totals = lax.map(
        attend_block, (by_block(queries), by_block(key_rows), by_block(values), labels)
    )
    attended = mixed.reshape(rows, width)
    residual = inputs + jnp.dot(attended, w_out, preferred_element_type=jnp.float32)
    scale_mlp = lax.rsqrt(jnp.mean(residual * residual, axis=-1, keepdims=True) + EPSILON)
    normed_mlp = (residual * scale_mlp * gain_mlp).astype(jnp.bfloat16)
    hidden = jnp.dot(normed_mlp, w_up, preferred_element_type=jnp.float32) + b_up
    activated, gelu_pullback = jax.vjp(tanh_gelu, hidden)
    active_low = activated.astype(jnp.bfloat16)
    layer_out = (
        residual + (jnp.dot(active_low, w_down, preferred_element_type=jnp.float32) + b_down)
    ).astype(jnp.bfloat16)
    grad_down = jnp.einsum("tf,td->fd", active_low, out_grad, preferred_element_type=jnp.float32)
    grad_downbias = jnp.sum(out_grad.astype(jnp.float32), axis=0)
    grad_active = jnp.einsum("td,fd->tf", out_grad, w_down, preferred_element_type=jnp.float32)
    grad_hidden = gelu_pullback(grad_active)[0].astype(jnp.bfloat16)
    grad_upbias = jnp.sum(grad_hidden.astype(jnp.float32), axis=0)
    grad_up = jnp.einsum("td,tf->df", normed_mlp, grad_hidden, preferred_element_type=jnp.float32)
    grad_normed_mlp = jnp.einsum("tf,df->td", grad_hidden, w_up, preferred_element_type=jnp.float32)
    residual_part, grad_gainmlp = norm_back(residual, scale_mlp, gain_mlp, grad_normed_mlp)
    grad_residual = out_grad.astype(jnp.float32) + residual_part
    grad_branch = grad_residual.astype(jnp.bfloat16)
    grad_outproj = jnp.einsum(
        "ta,td->ad", attended, grad_branch, preferred_element_type=jnp.float32
    )
    grad_attended = jnp.einsum(
        "td,ad->ta", grad_branch, w_out, preferred_element_type=jnp.float32
    ).astype(jnp.bfloat16)
    grad_queries, grad_keys, grad_values = lax.map(
        attend_back,
        (
            by_block(queries),
            by_block(key_rows),
            by_block(values),
            labels,
            by_block(grad_attended.reshape(rows, heads, head_dim)),
            log_totals,
        ),
    )
    query_back = (
        rotate_back(grad_queries.reshape(rows, heads, head_dim) * scaling, cos_table, sin_table)
        .reshape(rows, width)
        .astype(jnp.bfloat16)
    )
    key_back = (
        rotate_back(grad_keys.reshape(rows, heads, head_dim), cos_table, sin_table)
        .reshape(rows, width)
        .astype(jnp.bfloat16)
    )
    value_back = grad_values.reshape(rows, width).astype(jnp.bfloat16)
    grad_query = jnp.einsum(
        "td,ta->da", normed_attn, query_back, preferred_element_type=jnp.float32
    )
    grad_key = jnp.einsum("td,ta->da", normed_attn, key_back, preferred_element_type=jnp.float32)
    grad_value = jnp.einsum(
        "td,ta->da", normed_attn, value_back, preferred_element_type=jnp.float32
    )
    grad_normed_attn = jnp.einsum(
        "ta,da->td", query_back, w_query, preferred_element_type=jnp.float32
    )
    grad_normed_attn = grad_normed_attn + jnp.einsum(
        "ta,da->td", key_back, w_key, preferred_element_type=jnp.float32
    )
    grad_normed_attn = grad_normed_attn + jnp.einsum(
        "ta,da->td", value_back, w_value, preferred_element_type=jnp.float32
    )
    input_part, grad_gainattn = norm_back(inputs, scale_attn, gain_attn, grad_normed_attn)
    grad_tokens = (grad_residual + input_part).astype(jnp.bfloat16)
    totals = summed(grad_query, grad_key, grad_value, grad_outproj, grad_up, grad_upbias, grad_down)
    small = lax.psum((grad_downbias, grad_gainattn, grad_gainmlp), ("dp", "sub"))
    return (
        layer_out,
        grad_tokens,
        totals[0],
        totals[1],
        totals[2],
        totals[3],
        totals[4],
        totals[5],
        totals[6],
        small[0],
        small[1],
        small[2],
    )


def solution(mesh):
    in_specs = (
        P(("dp", "sub"), None),
        P(("dp", "sub")),
        P(("dp", "sub")),
        P(("dp", "sub"), None),
        P(),
        P(),
        P(),
        P(),
        P(),
        P(),
        P(),
        P(),
        P(),
        P(),
    )
    out_specs = (
        P(("dp", "sub"), None),
        P(("dp", "sub"), None),
        P(),
        P(),
        P(),
        P(),
        P(),
        P(),
        P(),
        P(),
        P(),
        P(),
    )
    return jax.shard_map(body, mesh=mesh, in_specs=in_specs, out_specs=out_specs, check_vma=False)
```

```python
import functools
import math

import jax
import jax.numpy as jnp
from jax import lax
from jax.experimental import pallas as pl
from jax.experimental.pallas import tpu as pltpu
from jax.sharding import Mesh
from jax.sharding import PartitionSpec as P

HEAD = 64
BLK = 512
EPSILON = 1e-06
TILE = 64
WINDOW = 2 * TILE
GROUP = 4
LANES = GROUP * HEAD
ROWS = 256
FFT = 256
F32 = jnp.float32
BF16 = jnp.bfloat16
GELU_A = math.sqrt(2.0 / math.pi)
GELU_B = 0.044715
VMEM_LIMIT = 56 * 1024 * 1024


def dot(a, b):
    return lax.dot_general(a, b, (((1,), (0,)), ((), ())), preferred_element_type=F32)


def dot_nt(a, b):
    return lax.dot_general(a, b, (((1,), (1,)), ((), ())), preferred_element_type=F32)


def dot_tn(a, b):
    return lax.dot_general(a, b, (((0,), (0,)), ((), ())), preferred_element_type=F32)


def cost(flops, moved, transcendentals=0):
    return pl.CostEstimate(
        flops=int(flops), bytes_accessed=int(moved), transcendentals=int(transcendentals)
    )


def params(axes=1):
    return pltpu.CompilerParams(
        dimension_semantics=("arbitrary",) * axes, vmem_limit_bytes=VMEM_LIMIT
    )


def partner(u):
    lane = lax.broadcasted_iota(jnp.int32, u.shape, 1)
    return jnp.where(lane % HEAD < HEAD // 2, pltpu.roll(u, 96, 1), pltpu.roll(u, 32, 1))


def head_masks(dtype):
    lane = lax.broadcasted_iota(jnp.int32, (TILE, LANES), 1)
    return [(lane // HEAD == h).astype(F32).astype(dtype) for h in range(GROUP)]


def spread(values, masks):
    return jnp.concatenate([values * mask for mask in masks], axis=0)


def gather_heads(stacked, masks):
    total = stacked[:TILE] * masks[0]
    for h in range(1, GROUP):
        total = total + stacked[h * TILE : (h + 1) * TILE] * masks[h]
    return total


def attention_kernel(
    x_ref, cos_ref, sin_ref, seg_ref, ga_ref, gm_ref, wq_ref, wk_ref, wv_ref, wo_ref,
    n1_ref, q_ref, k_ref, v_ref, p_ref, att_ref, x1_ref, n2_ref, keys, vals,
):
    i = pl.program_id(0)
    width = x_ref.shape[1]
    x = x_ref[...].astype(F32)
    scale = lax.rsqrt(jnp.mean(x * x, axis=-1, keepdims=True) + EPSILON)
    n1 = (x * scale * ga_ref[...]).astype(BF16)
    n1_ref[...] = n1
    here = pl.ds(pl.multiple_of(i * ROWS, ROWS), ROWS)
    cos_t, sin_t = cos_ref[...], sin_ref[...]
    query = dot(n1, wq_ref[...])
    key = dot(n1, wk_ref[...])
    value = dot(n1, wv_ref[...]).astype(BF16)
    v_ref[...] = value
    vals[here, :] = value
    for s in range(width // 128):
        at = slice(128 * s, 128 * s + 128)
        u = query[:, at]
        q_ref[:, at] = ((u * cos_t + partner(u) * sin_t) * (1.0 / math.sqrt(HEAD))).astype(BF16)
        u = key[:, at]
        turned = (u * cos_t + partner(u) * sin_t).astype(BF16)
        k_ref[:, at] = turned
        keys[here, at] = turned
    low_masks, masks = head_masks(BF16), head_masks(F32)
    per_block = BLK // ROWS
    base = (i // per_block) * BLK
    for t in range(ROWS // TILE):
        row0 = i * ROWS + t * TILE
        first = row0 - TILE
        if t == 0:
            first = jnp.where(i % per_block == 0, row0, first)
        first = pl.multiple_of(first, TILE)
        lane = lax.broadcasted_iota(jnp.int32, (TILE, WINDOW), 1) + (first - base)
        row = lax.broadcasted_iota(jnp.int32, (TILE, WINDOW), 0) + (row0 - base)
        at_rows = slice(t * TILE, t * TILE + TILE)
        allowed = (lane >= seg_ref[at_rows, :]) & (lane <= row)
        bias = jnp.where(allowed, 0.0, -1e30)
        bias = jnp.concatenate([bias] * GROUP, axis=0)
        for g in range(width // LANES):
            at = slice(LANES * g, LANES * g + LANES)
            scores = dot_nt(spread(q_ref[at_rows, at], low_masks), keys[pl.ds(first, WINDOW), at])
            scores = scores + bias
            highest = jnp.max(scores, axis=-1, keepdims=True)
            weights = jnp.exp(scores - highest)
            share = weights * (1.0 / jnp.sum(weights, axis=-1, keepdims=True))
            part = (t * (width // LANES) + g) * GROUP * TILE
            p_ref[part : part + GROUP * TILE, :] = share
            mixed = dot(share.astype(BF16), vals[pl.ds(first, WINDOW), at])
            att_ref[at_rows, at] = gather_heads(mixed, masks).astype(BF16)
    x1 = x + dot(att_ref[...], wo_ref[...])
    x1_ref[...] = x1
    scale = lax.rsqrt(jnp.mean(x1 * x1, axis=-1, keepdims=True) + EPSILON)
    n2_ref[...] = (x1 * scale * gm_ref[...]).astype(BF16)


def attention_forward(tokens, cos_t, sin_t, seg, gain_attn, gain_mlp, wq, wk, wv, wo):
    rows, width = tokens.shape
    tile = pl.BlockSpec((ROWS, width), lambda i: (i, 0))
    table = pl.BlockSpec((ROWS, 128), lambda i: (i, 0))
    gain = pl.BlockSpec((1, width), lambda i: (0, 0))
    weight = pl.BlockSpec((width, width), lambda i: (0, 0), pipeline_mode=pl.Buffered(1))
    shares = rows * (width // LANES) * GROUP
    low = jax.ShapeDtypeStruct((rows, width), BF16)
    return pl.pallas_call(
        attention_kernel,
        grid=(rows // ROWS,),
        in_specs=[tile, table, table, table, gain, gain, weight, weight, weight, weight],
        out_specs=[tile, tile, tile, tile,
                   pl.BlockSpec((shares * ROWS // rows, WINDOW), lambda i: (i, 0)),
                   tile, tile, tile],
        out_shape=[low, low, low, low, jax.ShapeDtypeStruct((shares, WINDOW), F32), low,
                   jax.ShapeDtypeStruct((rows, width), F32), low],
        scratch_shapes=[pltpu.VMEM((rows, width), BF16), pltpu.VMEM((rows, width), BF16)],
        compiler_params=params(),
        cost_estimate=cost(12 * rows * width * width, 30 * rows * width + 8 * width * width,
                           2 * shares * WINDOW),
        name="attention_forward",
    )(tokens, cos_t, sin_t, seg, gain_attn, gain_mlp, wq, wk, wv, wo)


def mlp_kernel(quarter, n2_ref, g_ref, wu_ref, bu_ref, wd_ref, *rest):
    d_ref, u_ref, act_ref, dh_ref, ub_ref = rest[-5:]
    rows = n2_ref.shape[0]
    total = jnp.zeros((1, FFT), F32)
    for r in range(rows // ROWS):
        at = slice(r * ROWS, r * ROWS + ROWS)
        h = dot(n2_ref[at, :], wu_ref[...]) + bu_ref[...]
        square = h * h
        tanh = jnp.tanh(h * (GELU_A + (GELU_A * GELU_B) * square))
        half = 0.5 * h
        act_ref[at, :] = (half + half * tanh).astype(BF16)
        slope = (0.5 + 0.5 * tanh) + half * (1.0 - tanh * tanh) * (
            GELU_A + (3.0 * GELU_A * GELU_B) * square
        )
        dh = (dot_nt(g_ref[at, :], wd_ref[...]) * slope).astype(BF16)
        dh_ref[at, :] = dh
        total = total + jnp.sum(dh.astype(F32), axis=0, keepdims=True)
    ub_ref[...] = total
    d_ref[...] = dot_tn(act_ref[...], g_ref[...])
    u_ref[...] = dot_tn(n2_ref[...], dh_ref[...])


def mlp_quarter(quarter, n2, grad, w_up, b_up, w_down, carried):
    rows, width = n2.shape
    wide = w_up.shape[1]
    steps = wide // 4 // FFT
    full = pl.BlockSpec((rows, width), lambda t, q: (0, 0), pipeline_mode=pl.Buffered(1))
    columns = pl.BlockSpec((rows, FFT), lambda t, q: (0, q[0] * steps + t))
    line = pl.BlockSpec((1, FFT), lambda t, q: (0, q[0] * steps + t))
    low = jax.ShapeDtypeStruct((rows, wide), BF16)
    aliases = {6 + n: 2 + n for n in range(len(carried))}
    return pl.pallas_call(
        mlp_kernel,
        grid_spec=pltpu.PrefetchScalarGridSpec(
            num_scalar_prefetch=1,
            grid=(steps,),
            in_specs=[full, full,
                      pl.BlockSpec((width, FFT), lambda t, q: (0, q[0] * steps + t)),
                      line,
                      pl.BlockSpec((FFT, width), lambda t, q: (q[0] * steps + t, 0))]
            + [pl.BlockSpec(memory_space=pl.ANY)] * len(carried),
            out_specs=[pl.BlockSpec((FFT, width), lambda t, q: (t, 0)),
                       pl.BlockSpec((width, FFT), lambda t, q: (0, t)),
                       columns, columns, line],
        ),
        out_shape=[jax.ShapeDtypeStruct((wide // 4, width), F32),
                   jax.ShapeDtypeStruct((width, wide // 4), F32),
                   low, low, jax.ShapeDtypeStruct((1, wide), F32)],
        input_output_aliases=aliases,
        compiler_params=params(),
        cost_estimate=cost(8 * rows * width * wide // 4, 4 * rows * width + 4 * width * wide,
                           rows * wide // 4),
        name="mlp_quarter",
    )(quarter, n2, grad, w_up, b_up, w_down, *carried)


def back_kernel(dh_ref, wu_ref, x1_ref, g_ref, gm_ref, wo_ref, dx1_ref, db_ref, do_ref, sums_ref):
    x1 = x1_ref[...]
    g = g_ref[...].astype(F32)
    scale = lax.rsqrt(jnp.mean(x1 * x1, axis=-1, keepdims=True) + EPSILON)
    dn2 = dot_nt(dh_ref[...], wu_ref[...])
    weighted = dn2 * gm_ref[...]
    dot_x = jnp.mean(weighted * x1, axis=-1, keepdims=True)
    dx1 = g + (scale * weighted - x1 * ((scale * scale * scale) * dot_x))
    dx1_ref[...] = dx1
    db = dx1.astype(BF16)
    db_ref[...] = db
    do_ref[...] = dot_nt(db, wo_ref[...]).astype(BF16)

    @pl.when(pl.program_id(0) == 0)
    def _():
        sums_ref[...] = jnp.zeros_like(sums_ref)

    sums_ref[0:1, :] += jnp.sum(dn2 * (x1 * scale), axis=0, keepdims=True)
    sums_ref[1:2, :] += jnp.sum(g, axis=0, keepdims=True)


def back_to_attention(dh, w_up, x1, grad, gain_mlp, w_out):
    rows, width = x1.shape
    wide = w_up.shape[1]
    tile = pl.BlockSpec((ROWS, width), lambda i: (i, 0))
    low = jax.ShapeDtypeStruct((rows, width), BF16)
    return pl.pallas_call(
        back_kernel,
        grid=(rows // ROWS,),
        in_specs=[pl.BlockSpec((ROWS, wide), lambda i: (i, 0)),
                  pl.BlockSpec((width, wide), lambda i: (0, 0), pipeline_mode=pl.Buffered(1)),
                  tile, tile,
                  pl.BlockSpec((1, width), lambda i: (0, 0)),
                  pl.BlockSpec((width, width), lambda i: (0, 0), pipeline_mode=pl.Buffered(1))],
        out_specs=[tile, tile, tile, pl.BlockSpec((8, width), lambda i: (0, 0))],
        out_shape=[jax.ShapeDtypeStruct((rows, width), F32), low, low,
                   jax.ShapeDtypeStruct((8, width), F32)],
        compiler_params=params(),
        cost_estimate=cost(2 * rows * width * (wide + width),
                           rows * (2 * wide + 14 * width) + 2 * width * (wide + width)),
        name="back_to_attention",
    )(dh, w_up, x1, grad, gain_mlp, w_out)


def attention_back_kernel(
    q_ref, k_ref, v_ref, do_ref, p_ref, cos_ref, sin_ref, qg_ref, kg_ref, vg_ref, dk, dv
):
    width = q_ref.shape[1]
    groups = width // LANES
    low_masks, masks = head_masks(BF16), head_masks(F32)
    dk[...] = jnp.zeros_like(dk)
    dv[...] = jnp.zeros_like(dv)
    for t in range(BLK // TILE):
        at_rows = slice(t * TILE, t * TILE + TILE)
        first = max(t - 1, 0) * TILE
        window = slice(first, first + WINDOW)
        for g in range(groups):
            at = slice(LANES * g, LANES * g + LANES)
            share = p_ref[(t * groups + g) * GROUP * TILE : (t * groups + g + 1) * GROUP * TILE, :]
            low = share.astype(BF16)
            d_out = spread(do_ref[at_rows, at], low_masks)
            queries = spread(q_ref[at_rows, at], low_masks)
            d_share = dot_nt(d_out, v_ref[window, at])
            row_dot = jnp.sum(d_share * share, axis=-1, keepdims=True)
            d_score = (share * (d_share - row_dot)).astype(BF16)
            dv[window, at] += dot_tn(low, d_out)
            dk[window, at] += dot_tn(d_score, queries)
            dq = gather_heads(dot(d_score, k_ref[window, at]), masks)
            dq = dq * (1.0 / math.sqrt(HEAD))
            for s in range(LANES // 128):
                u = dq[:, 128 * s : 128 * s + 128]
                turned = u * cos_ref[at_rows, :] - partner(u) * sin_ref[at_rows, :]
                qg_ref[at_rows, LANES * g + 128 * s : LANES * g + 128 * s + 128] = turned.astype(BF16)
    vg_ref[...] = dv[...].astype(BF16)
    cos_t, sin_t = cos_ref[...], sin_ref[...]
    for s in range(width // 128):
        at = slice(128 * s, 128 * s + 128)
        u = dk[:, at]
        kg_ref[:, at] = (u * cos_t - partner(u) * sin_t).astype(BF16)


def attention_backward(q, k, v, d_out, shares, cos_t, sin_t):
    rows, width = q.shape
    tile = pl.BlockSpec((BLK, width), lambda i: (i, 0))
    table = pl.BlockSpec((BLK, 128), lambda i: (i, 0))
    low = jax.ShapeDtypeStruct((rows, width), BF16)
    count = shares.shape[0]
    return pl.pallas_call(
        attention_back_kernel,
        grid=(rows // BLK,),
        in_specs=[tile, tile, tile, tile,
                  pl.BlockSpec((count * BLK // rows, WINDOW), lambda i: (i, 0)), table, table],
        out_specs=[tile, tile, tile],
        out_shape=[low, low, low],
        scratch_shapes=[pltpu.VMEM((BLK, width), F32), pltpu.VMEM((BLK, width), F32)],
        compiler_params=params(),
        cost_estimate=cost(10 * count * WINDOW * LANES, 14 * rows * width + 4 * count * WINDOW),
        name="attention_backward",
    )(q, k, v, d_out, shares, cos_t, sin_t)


def weight_kernel(half, att_ref, n1_ref, db_ref, qg_ref, kg_ref, vg_ref, first_ref, second_ref):
    step = pl.program_id(0)
    for n, (left, right, out) in enumerate(
        ((att_ref, db_ref, first_ref), (n1_ref, qg_ref, first_ref),
         (n1_ref, kg_ref, second_ref), (n1_ref, vg_ref, second_ref))
    ):
        @pl.when(step == n)
        def _(left=left, right=right, out=out):
            out[...] = dot_tn(left[...], right[...])


def weight_half(half, att, n1, db, qg, kg, vg):
    rows, width = n1.shape
    full = pl.BlockSpec((rows, width), lambda k, h: (0, 0), pipeline_mode=pl.Buffered(1))
    left = pl.BlockSpec((rows, width // 2), lambda k, h: (0, h[0]), pipeline_mode=pl.Buffered(1))
    out = jax.ShapeDtypeStruct((width, width), F32)
    return pl.pallas_call(
        weight_kernel,
        grid_spec=pltpu.PrefetchScalarGridSpec(
            num_scalar_prefetch=1,
            grid=(4,),
            in_specs=[left, left, full, full, full, full],
            out_specs=[pl.BlockSpec((width // 2, width), lambda k, h: (jnp.minimum(k, 1), 0)),
                       pl.BlockSpec((width // 2, width), lambda k, h: (jnp.maximum(k - 2, 0), 0))],
        ),
        out_shape=[out, out],
        compiler_params=params(),
        cost_estimate=cost(4 * rows * width * width, 10 * rows * width + 8 * width * width),
        name="weight_half",
    )(half, att, n1, db, qg, kg, vg)


def tail_kernel(
    qg_ref, kg_ref, vg_ref, wq_ref, wk_ref, wv_ref, x_ref, dx1_ref, ga_ref,
    act_ref, wd_ref, x1_ref, bd_ref, gt_ref, lo_ref, sums_ref,
):
    dn1 = dot_nt(qg_ref[...], wq_ref[...])
    dn1 = dn1 + dot_nt(kg_ref[...], wk_ref[...])
    dn1 = dn1 + dot_nt(vg_ref[...], wv_ref[...])
    x = x_ref[...].astype(F32)
    scale = lax.rsqrt(jnp.mean(x * x, axis=-1, keepdims=True) + EPSILON)
    weighted = dn1 * ga_ref[...]
    dot_x = jnp.mean(weighted * x, axis=-1, keepdims=True)
    gt_ref[...] = (
        dx1_ref[...] + (scale * weighted - x * ((scale * scale * scale) * dot_x))
    ).astype(BF16)
    lo_ref[...] = (x1_ref[...] + (dot(act_ref[...], wd_ref[...]) + bd_ref[...])).astype(BF16)

    @pl.when(pl.program_id(0) == 0)
    def _():
        sums_ref[...] = jnp.zeros_like(sums_ref)

    sums_ref[0:1, :] += jnp.sum(dn1 * (x * scale), axis=0, keepdims=True)


def tail(qg, kg, vg, wq, wk, wv, tokens, dx1, gain_attn, act, w_down, x1, b_down):
    rows, width = tokens.shape
    wide = w_down.shape[0]
    tile = pl.BlockSpec((ROWS, width), lambda i: (i, 0))
    line = pl.BlockSpec((1, width), lambda i: (0, 0))
    weight = pl.BlockSpec((width, width), lambda i: (0, 0), pipeline_mode=pl.Buffered(1))
    low = jax.ShapeDtypeStruct((rows, width), BF16)
    return pl.pallas_call(
        tail_kernel,
        grid=(rows // ROWS,),
        in_specs=[tile, tile, tile, weight, weight, weight, tile, tile, line,
                  pl.BlockSpec((ROWS, wide), lambda i: (i, 0)),
                  pl.BlockSpec((wide, width), lambda i: (0, 0), pipeline_mode=pl.Buffered(1)),
                  tile, line],
        out_specs=[tile, tile, pl.BlockSpec((8, width), lambda i: (0, 0))],
        out_shape=[low, low, jax.ShapeDtypeStruct((8, width), F32)],
        compiler_params=params(),
        cost_estimate=cost(2 * rows * width * (3 * width + wide),
                           rows * (2 * wide + 20 * width) + 2 * width * (wide + 3 * width)),
        name="tail",
    )(qg, kg, vg, wq, wk, wv, tokens, dx1, gain_attn, act, w_down, x1, b_down)


AXES = ("dp", "sub")
CORE, X, Y, Z0, Z1 = 1, 2, 4, 8, 16
PLACES = 32


def swap(array, bit):
    return lax.ppermute(array, AXES, [(i, i ^ bit) for i in range(PLACES)])


def halve(kept, received, bit):
    size = kept.shape[0] // 2

    def part(index):
        return lax.dynamic_slice_in_dim(kept, index * size, size, 0) + (
            lax.dynamic_slice_in_dim(received, index * size, size, 0)
        )

    return part(bit), part(1 - bit)


def shard_sum(place, first, second):
    bit = {b: (place // b) % 2 for b in (X, Y, Z0, Z1)}
    (keep1, send1), (keep2, send2) = first, second
    keep1, send1 = halve(keep1, swap(send1, CORE), bit[X])
    keep2, send2 = halve(keep2, swap(send2, CORE), bit[Y])
    keep1, send1 = halve(keep1, swap(send1, X), bit[Z0])
    keep2, send2 = halve(keep2, swap(send2, Y), bit[Z0])
    received = swap(jnp.concatenate([send1, send2], axis=0), Z0)
    size = keep1.shape[0]
    keep1, send1 = halve(keep1, received[:size], bit[Y])
    keep2, send2 = halve(keep2, received[size:], bit[X])
    keep1, send1 = halve(keep1, swap(send1, Y), bit[Z1])
    keep2, send2 = halve(keep2, swap(send2, X), bit[Z1])
    received = swap(jnp.concatenate([send1, send2], axis=0), Z1)
    return jnp.concatenate([keep1, keep2], axis=0) + received


def offsets(device, rows):
    bits = [(device // b) % 2 for b in (X, Y, Z0, Z1)]
    x, y, z0, z1 = bits
    unit = rows // 16
    return unit * (8 * x + 4 * z0 + 2 * y + z1), unit * (8 * y + 4 * z0 + 2 * x + z1)


def place_mlp_kernel(chunk, gathered, *rest):
    down, up, sems = rest[-3:]
    rows = gathered.shape[1] // 2
    width = gathered.shape[2]
    copies = []
    for device in range(PLACES):
        at1, at2 = offsets(device, rows * 16)
        quarter = 2 * chunk + device % 2
        copies.append(pltpu.make_async_copy(
            gathered.at[device, pl.ds(0, rows), :],
            down.at[pl.ds(quarter * width + at1, rows), :], sems.at[2 * device]))
        copies.append(pltpu.make_async_copy(
            gathered.at[device, pl.ds(rows, rows), :],
            up.at[pl.ds(at2, rows), pl.ds(quarter * width, width)], sems.at[2 * device + 1]))
    for copy in copies:
        copy.start()
    for copy in copies:
        copy.wait()


def place_mlp(chunk, gathered, wide, carried):
    width = gathered.shape[2]
    return pl.pallas_call(
        functools.partial(place_mlp_kernel, chunk),
        in_specs=[pl.BlockSpec(memory_space=pl.ANY)] * (1 + len(carried)),
        out_specs=[pl.BlockSpec(memory_space=pl.ANY)] * 2,
        out_shape=[jax.ShapeDtypeStruct((wide, width), F32),
                   jax.ShapeDtypeStruct((width, wide), F32)],
        input_output_aliases={1 + n: n for n in range(len(carried))},
        scratch_shapes=[pltpu.SemaphoreType.DMA((2 * PLACES,))],
        cost_estimate=cost(0, 8 * gathered.size),
        name="place_mlp",
    )(gathered, *carried)


def place_rest_kernel(gathered, outproj, query, key, value, sems):
    rows = gathered.shape[1] // 2
    width = gathered.shape[2]
    copies = []
    for device in range(PLACES):
        at1, at2 = offsets(device, rows * 16)
        half = (device % 2) * (width // 2)
        for n, (at, pair) in enumerate(((at1, (outproj, query)), (at2, (key, value)))):
            target = pair[at // (width // 2)]
            copies.append(pltpu.make_async_copy(
                gathered.at[device, pl.ds(n * rows, rows), :],
                target.at[pl.ds(half + at % (width // 2), rows), :], sems.at[2 * device + n]))
    for copy in copies:
        copy.start()
    for copy in copies:
        copy.wait()


def place_rest(gathered):
    width = gathered.shape[2]
    return pl.pallas_call(
        place_rest_kernel,
        in_specs=[pl.BlockSpec(memory_space=pl.ANY)],
        out_specs=[pl.BlockSpec(memory_space=pl.ANY)] * 4,
        out_shape=[jax.ShapeDtypeStruct((width, width), F32)] * 4,
        scratch_shapes=[pltpu.SemaphoreType.DMA((2 * PLACES,))],
        cost_estimate=cost(0, 8 * gathered.size),
        name="place_rest",
    )(gathered)


def body(
    replicas, tokens, segment_ids, positions, out_grad, w_query, w_key, w_value, w_out,
    w_up, b_up, w_down, b_down, gain_attn, gain_mlp,
):
    wide = w_up.shape[1]
    place = lax.axis_index("dp") * 4 + lax.axis_index("sub")
    core = place % 2

    def index(value):
        return jnp.asarray(value, jnp.int32).reshape(1)

    half_dim = HEAD // 2
    lane = jnp.arange(128, dtype=jnp.int32)
    frequency = jnp.exp(
        (lane % half_dim).astype(F32) * (-math.log(10000.0) / half_dim)
    )
    phases = positions.astype(F32)[:, None] * frequency[None, :]
    cos_t = jnp.cos(phases)
    sin_t = jnp.sin(phases) * jnp.where(lane % HEAD < half_dim, -1.0, 1.0)[None, :]
    seg = jnp.broadcast_to(segment_ids[:, None], phases.shape)
    gain_attn, gain_mlp, b_down, b_up = (
        v.reshape(1, -1) for v in (gain_attn, gain_mlp, b_down, b_up)
    )

    n1, q, k, v, shares, att, x1, n2 = attention_forward(
        tokens, cos_t, sin_t, seg, gain_attn, gain_mlp, w_query, w_key, w_value, w_out
    )
    carried = ()
    chunks = []
    for chunk in range(2):
        parts = []
        for owner in (1 - core, core):
            down, up, *carried = mlp_quarter(
                index(2 * chunk + owner), n2, out_grad, w_up, b_up, w_down, tuple(carried)
            )
            parts.append((down, up))
        (down_sent, up_sent), (down_kept, up_kept) = parts
        chunks.append(shard_sum(place, (down_kept, down_sent), (up_kept, up_sent)))
    act, dh, up_bias = carried
    dx1, db, d_out, sums1 = back_to_attention(dh, w_up, x1, out_grad, gain_mlp, w_out)
    qg, kg, vg = attention_backward(q, k, v, d_out, shares, cos_t, sin_t)
    sent1, sent2 = weight_half(index(1 - core), att, n1, db, qg, kg, vg)
    kept1, kept2 = weight_half(index(core), att, n1, db, qg, kg, vg)
    chunks.append(shard_sum(place, (kept1, sent1), (kept2, sent2)))
    grad_tokens, layer_out, sums2 = tail(
        qg, kg, vg, w_query, w_key, w_value, tokens, dx1, gain_attn, act, w_down, x1, b_down
    )
    small = jnp.concatenate([sums1[0:2], sums2[0:1], up_bias.reshape(wide // sums1.shape[1], -1)])
    small = lax.psum(small, AXES)
    if replicas:
        small = lax.psum(small, "rep")
        chunks = [lax.psum(chunk, "rep") for chunk in chunks]
    gathered = [lax.all_gather(chunk, AXES) for chunk in chunks]
    placed = place_mlp(0, gathered[0], wide, ())
    grad_down, grad_up = place_mlp(1, gathered[1], wide, tuple(placed))
    grad_outproj, grad_query, grad_key, grad_value = place_rest(gathered[2])
    return (
        layer_out, grad_tokens, grad_query, grad_key, grad_value, grad_outproj, grad_up,
        small[3:].reshape(-1), grad_down, small[1], small[2], small[0],
    )


def solution(mesh):
    dp, sub = mesh.shape["dp"], mesh.shape["sub"]
    groups = dp * sub // PLACES
    split = ("dp", "sub")
    if groups > 1:
        mesh = Mesh(mesh.devices.reshape(groups, PLACES // sub, sub), ("rep", "dp", "sub"))
        split = ("rep", "dp", "sub")
    in_specs = (P(split, None), P(split), P(split), P(split, None)) + (P(),) * 10
    out_specs = (P(split, None), P(split, None)) + (P(),) * 10
    return jax.shard_map(
        functools.partial(body, groups > 1),
        mesh=mesh, in_specs=in_specs, out_specs=out_specs, check_vma=False,
    )
```
